32 devices in a mesh: rep: 4 (over z), tp: 2 (over x), seq: 4 (over y, core).
Axes of the slice: x: 2, y: 2, z: 4, core: 2. Of those that a mesh axis runs over, the one named last changes fastest.
Arguments:
- prompt_x: bfloat16 [4, 4096, 8192], P('rep', 'seq'), may hold values from -6 to 6
- norm_gain: float32 [8192], replicated, may hold values from 0.1 to 1.9
- key_weight: bfloat16 [8192, 1024], P(None, 'tp'), may hold values from -0.0625 to 0.0625
- value_weight: bfloat16 [8192, 1024], P(None, 'tp'), may hold values from -0.0625 to 0.0625
- prompt_lengths: int32 [4], replicated, may hold values from 1024 to 4096
- page_table: int32 [4, 32], replicated, may hold values from 0 to 127, as said below
- request_slots: int32 [128], replicated, may hold values from 0 to 3
- queries: bfloat16 [4, 128, 8192], P(None, None, 'tp'), may hold values from -240 to 240
- new_kv: bfloat16 [2, 4, 128, 1024], P(None, None, ('rep', 'seq')), may hold values from -6 to 6
Outputs:
- attention: bfloat16 [4, 128, 8192], P(None, ('rep', 'seq'), 'tp')
- paged_cache: bfloat16 [128, 2, 128, 1024], P(('rep', 'seq'), None, None, 'tp')
The draws below stay inside these ranges and needn't reach their ends.
Inputs may be any that keep to these rules, and one draw needn't show every extreme that they name: `page_table`: every page 0 to 127 is named once; page // 8 is the decode shard (index of rep times 4 plus index of seq) that holds it; the blocks b * 8 to b * 8 + 7 of one prompt go to 8 different shards. `request_slots`: several requests may continue one prompt. `prompt_lengths`: tokens at or past a prompt's length are padding.
All inputs are finite; a program needn't handle non-finite values.
Results may differ from the reference program's by a relative error of at most 0.02.
The reference program's roundings to bfloat16 on the way count: a program that leaves them out, or rounds other values in their place, can miss the bound.
Values may be sent and summed in bfloat16 or wider, within the bound.
A program may use at most 192 MiB of HBM per device.

```python
import jax
import jax.numpy as jnp
from jax import lax

D = 8192
QH = 64
KVH = 8
HD = 128
BLK = 128
BPD = 8
STEPS = 4
PROMPTS = 4
SHARDS = 16
REPL = 1
KV_COLS = 1024
BLOCKS = 32
PLEN = 4096
PAGES = 128
REQS = 128


def draw_page_table(key, part):
    first_key, second_key, third_key = jax.random.split(jax.random.fold_in(key, 11), 3)
    order_dest = jax.random.permutation(first_key, SHARDS)
    order_src = jax.random.permutation(second_key, SHARDS)
    slot_order = jax.random.permutation(third_key, jnp.tile(jnp.arange(BPD, dtype=jnp.int32), (SHARDS, 1)), axis=1, independent=True)
    targets = order_dest[(order_src[:, None] + slot_order) % SHARDS]
    return (targets * BPD + slot_order).reshape(PROMPTS, BLOCKS).astype(jnp.int32)


def draw_queries(key, part):
    base_key = jax.random.fold_in(jax.random.fold_in(key, 23), 0)
    drawn = jax.random.truncated_normal(base_key, -6.0, 6.0, (STEPS, REQS, QH * HD), jnp.float32)
    return drawn.astype(jnp.bfloat16)


def touch_ends(entries, rng, low, high):
    longest = entries.shape.index(max(entries.shape))
    spots = []
    for shift in (0, 1):
        where = [jax.random.randint(jax.random.fold_in(rng, axis), (), 0, length) for axis, length in enumerate(entries.shape)]
        where[longest] = (where[longest] + shift) % entries.shape[longest]
        spots.append(tuple(where))
    return entries.at[spots[0]].set(low).at[spots[1]].set(high)


def levels(key, shape, pieces, low, top_value):
    def one(position, parts):
        draws = jax.random.uniform(jax.random.fold_in(jax.random.fold_in(key, 6), position), (parts,), jnp.float32, low / len(pieces), top_value / len(pieces))
        return jnp.repeat(jnp.exp(draws), shape[position] // parts).reshape((-1,) + (1,) * (len(shape) - position - 1))

    factor_of = one(*pieces[0])
    for cut in pieces[1:]:
        factor_of = factor_of * one(*cut)
    return factor_of


def noise(own_key, extent, deviation, most, cuts=(), held_as=jnp.bfloat16):
    values = deviation * jax.random.normal(own_key, extent, jnp.float32)
    if cuts:
        values = values * levels(own_key, extent, cuts, -0.22, 0.18)
    return jnp.clip(values, -most, most).astype(held_as)


def setup_inputs(seed: int = 0) -> dict:
    key_of = jax.random.split(jax.random.key(seed), 10)
    prompt_x = noise(key_of[0], (PROMPTS, PLEN, D), 1.0, 6.0, ((0, 4), (1, 4)))
    norm_gain = jnp.clip(1.0 + 0.18 * jax.random.normal(key_of[1], (D,), jnp.float32), 0.1, 1.9)
    key_weight = noise(key_of[2], (D, KVH * HD), D ** -0.5, 0.0625, ((1, 2),))
    value_weight = noise(key_of[3], (D, KVH * HD), D ** -0.5, 0.0625, ((1, 2),))
    prompt_lengths = touch_ends(jax.random.randint(key_of[4], (PROMPTS,), PLEN // 4, PLEN + 1), jax.random.fold_in(key_of[4], 1), PLEN // 4, PLEN).astype(jnp.int32)
    page_table = draw_page_table(jax.random.fold_in(key_of[9], 71), 0)
    request_slots = touch_ends(jax.random.randint(key_of[6], (REQS,), 0, PROMPTS), jax.random.fold_in(key_of[6], 1), 0, PROMPTS - 1).astype(jnp.int32)
    queries = draw_queries(jax.random.fold_in(key_of[9], 71), 0)
    new_kv = noise(key_of[8], (2, STEPS, REQS, KVH * HD), 1.0, 6.0, ((2, 16),))
    return dict(prompt_x=prompt_x, norm_gain=norm_gain, key_weight=key_weight, value_weight=value_weight, prompt_lengths=prompt_lengths, page_table=page_table, request_slots=request_slots, queries=queries, new_kv=new_kv)


rope_base = 500000.0
eps_norm = 1e-05

def rotate(values_in, positions, col_start, head_size):
    half_cols = values_in.shape[-1] // 2
    columns = col_start + 2 * jnp.arange(half_cols, dtype=jnp.int32)
    within = (columns % head_size).astype(jnp.float32)
    inverse = jnp.exp(-(within / head_size) * jnp.log(jnp.float32(rope_base)))
    angles = positions[..., None] * inverse
    cosine = jnp.cos(angles)
    sine_part = jnp.sin(angles)
    paired = values_in.reshape(values_in.shape[:-1] + (half_cols, 2))
    even_part = paired[..., 0]
    odd_part = paired[..., 1]
    turned = jnp.stack([even_part * cosine - odd_part * sine_part, even_part * sine_part + odd_part * cosine], -1)
    return turned.reshape(values_in.shape)

def widen(rows):
    split_rows = rows.reshape(PROMPTS, PLEN, KVH, 1, HD)
    copied = jnp.broadcast_to(split_rows, (PROMPTS, PLEN, KVH, REPL, HD))
    return copied.reshape(PROMPTS, PLEN, KV_COLS)

def round_weights(weights):
    return lax.optimization_barrier(weights.astype(jnp.bfloat16)).astype(jnp.float32)

def reference(prompt_x, norm_gain, key_weight, value_weight, prompt_lengths, page_table, request_slots, queries, new_kv):
    floated = prompt_x.astype(jnp.float32)
    square_mean = lax.optimization_barrier(jnp.mean(floated * floated, axis=-1, keepdims=True))
    normed = (floated * lax.rsqrt(square_mean + eps_norm) * norm_gain).astype(jnp.bfloat16)
    flat_rows = normed.reshape(PROMPTS * PLEN, D)
    key_rows = jnp.dot(flat_rows, key_weight, preferred_element_type=jnp.float32).reshape(PROMPTS, PLEN, KVH * HD)
    value_rows = jnp.dot(flat_rows, value_weight, preferred_element_type=jnp.float32).reshape(PROMPTS, PLEN, KVH * HD)
    value_rows = value_rows.astype(jnp.bfloat16)
    prompt_pos = jnp.arange(PLEN, dtype=jnp.int32).astype(jnp.float32)
    key_rows = rotate(key_rows, prompt_pos[None, :], 0, HD).astype(jnp.bfloat16)
    stacked = jnp.stack([widen(key_rows), widen(value_rows)], axis=1).reshape(PROMPTS, 2, BLOCKS, BLK, KV_COLS)
    blocks = stacked.transpose(0, 2, 1, 3, 4).reshape(PROMPTS * BLOCKS, 2, BLK, KV_COLS)
    paged_cache = jnp.zeros((PAGES, 2, BLK, KV_COLS), jnp.bfloat16).at[page_table.reshape(-1)].set(blocks)
    slot_len = prompt_lengths[request_slots]
    step_pos = (slot_len[None, :] + jnp.arange(STEPS, dtype=jnp.int32)[:, None]).astype(jnp.float32)
    rotated_q = rotate(queries.astype(jnp.float32), step_pos, 0, HD).astype(jnp.bfloat16)
    fresh_keys = rotate(new_kv[0].astype(jnp.float32), step_pos, 0, HD).astype(jnp.bfloat16)
    fresh_values = new_kv[1]
    group_size = QH // KVH
    score_scale = HD ** (-0.5)
    token_idx = jnp.arange(PLEN, dtype=jnp.int32)
    causal = jnp.arange(STEPS, dtype=jnp.int32)[None, :] <= jnp.arange(STEPS, dtype=jnp.int32)[:, None]
    highest = lax.Precision.HIGHEST

    def per_request(request):
        prompt = request_slots[request]
        length = prompt_lengths[prompt]
        cached_k = key_rows[prompt].astype(jnp.float32).reshape(PLEN, KVH, HD)
        cached_v = value_rows[prompt].astype(jnp.float32).reshape(PLEN, KVH, HD)
        query_rows = rotated_q[:, request].astype(jnp.float32).reshape(STEPS, KVH, group_size, HD)
        own_keys = fresh_keys[:, request].astype(jnp.float32).reshape(STEPS, KVH, HD)
        own_values = fresh_values[:, request].astype(jnp.float32).reshape(STEPS, KVH, HD)
        past_scores = jnp.einsum('tkgd,skd->tkgs', query_rows, cached_k, precision=highest) * score_scale
        recent_scores = jnp.einsum('tkgd,ukd->tkgu', query_rows, own_keys, precision=highest) * score_scale
        visible = (token_idx < length)[None, None, None, :]
        allowed = causal[:, None, None, :]
        row_peak = jnp.maximum(lax.optimization_barrier(jnp.max(jnp.where(visible, past_scores, -1e+30), axis=-1)), lax.optimization_barrier(jnp.max(jnp.where(allowed, recent_scores, -1e+30), axis=-1)))
        past_w = jnp.where(visible, jnp.exp(past_scores - row_peak[..., None]), 0.0)
        recent_w = jnp.where(allowed, jnp.exp(recent_scores - row_peak[..., None]), 0.0)
        row_total = lax.optimization_barrier(jnp.sum(past_w, axis=-1)) + lax.optimization_barrier(jnp.sum(recent_w, axis=-1))
        weighted = jnp.einsum('tkgs,skd->tkgd', round_weights(past_w), cached_v, precision=highest)
        weighted = weighted + jnp.einsum('tkgu,ukd->tkgd', round_weights(recent_w), own_values, precision=highest)
        return (weighted / row_total[..., None]).reshape(STEPS, QH * HD)
    attended = lax.map(per_request, jnp.arange(REQS, dtype=jnp.int32))
    return (attended.transpose(1, 0, 2).astype(jnp.bfloat16), paged_cache)
```

```python
import functools

import jax
import jax.numpy as jnp
from jax import lax
from jax.experimental import pallas as pl
from jax.experimental.pallas import tpu as pltpu
from jax.sharding import PartitionSpec as P

KVH = 8
HD = 128
ROPE_BASE = 500000.0
EPS = 1e-05
VMEM_BYTES = 60 * 1024 * 1024


def swapped(value, axis, bit):
    mask = 2**bit
    pairs = [(source, source ^ mask) for source in range(lax.axis_size(axis))]
    return lax.ppermute(value, axis, pairs)


def rope_tables(positions):
    column = jnp.arange(HD, dtype=jnp.int32)
    within = (column - column % 2).astype(jnp.float32)
    inverse = jnp.exp(-(within / HD) * jnp.log(jnp.float32(ROPE_BASE)))
    angles = positions[:, None] * inverse[None, :]
    sign = jnp.where(column % 2 == 0, -1.0, 1.0)
    return jnp.cos(angles), jnp.sin(angles) * sign[None, :]


def turn(block, cosine, sine):
    lane = lax.broadcasted_iota(jnp.int32, block.shape, 1)
    neighbour = jnp.where(
        lane % 2 == 0, pltpu.roll(block, HD - 1, 1), pltpu.roll(block, 1, 1)
    )
    return block * cosine + neighbour * sine


def project_kernel(
    x_ref, gain_ref, wk_ref, wv_ref, cos_ref, sin_ref, pages_ref, heads_ref, key_acc, value_acc
):
    rows, width = x_ref.shape
    head_width = wk_ref.shape[1]
    depth = min(1024, width)
    steps = width // depth

    def squares(i, partial):
        chunk = x_ref[:, pl.ds(pl.multiple_of(i * depth, depth), depth)].astype(jnp.float32)
        chunk = chunk * chunk
        for j in range(depth // HD):
            partial = partial + chunk[:, j * HD : (j + 1) * HD]
        return partial

    partial = lax.fori_loop(0, steps, squares, jnp.zeros((rows, HD), jnp.float32))
    scale = lax.rsqrt(jnp.sum(partial, axis=1, keepdims=True) / width + EPS)
    key_acc[...] = jnp.zeros_like(key_acc)
    value_acc[...] = jnp.zeros_like(value_acc)

    def multiply(i, carry):
        part = pl.ds(pl.multiple_of(i * depth, depth), depth)
        normed = (x_ref[:, part].astype(jnp.float32) * scale * gain_ref[:, part]).astype(
            jnp.bfloat16
        )
        key_acc[...] += jnp.dot(normed, wk_ref[part, :], preferred_element_type=jnp.float32)
        value_acc[...] += jnp.dot(normed, wv_ref[part, :], preferred_element_type=jnp.float32)
        return carry

    lax.fori_loop(0, steps, multiply, 0)
    page = pages_ref.shape[2]
    for h in range(head_width // HD):
        cols = slice(h * HD, (h + 1) * HD)
        keys = turn(key_acc[:, cols], cos_ref[...], sin_ref[...]).astype(jnp.bfloat16)
        values = value_acc[:, cols].astype(jnp.bfloat16)
        heads_ref[h, 0] = keys
        heads_ref[h, 1] = values
        for b in range(rows // page):
            pages_ref[b, 0, :, cols] = keys[b * page : (b + 1) * page]
            pages_ref[b, 1, :, cols] = values[b * page : (b + 1) * page]


def project(x, gain, wk, wv, cosine, sine, page):
    tokens, width = x.shape
    head_width = wk.shape[1]
    heads = head_width // HD
    rows = min(256, tokens)
    return pl.pallas_call(
        project_kernel,
        grid=(tokens // rows,),
        in_specs=[
            pl.BlockSpec((rows, width), lambda i: (i, 0)),
            pl.BlockSpec((1, width), lambda i: (0, 0)),
            pl.BlockSpec((width, head_width), lambda i: (0, 0), pipeline_mode=pl.Buffered(1)),
            pl.BlockSpec((width, head_width), lambda i: (0, 0), pipeline_mode=pl.Buffered(1)),
            pl.BlockSpec((rows, HD), lambda i: (i, 0)),
            pl.BlockSpec((rows, HD), lambda i: (i, 0)),
        ],
        out_specs=[
            pl.BlockSpec((rows // page, 2, page, head_width), lambda i: (i, 0, 0, 0)),
            pl.BlockSpec((heads, 2, rows, HD), lambda i: (0, 0, i, 0)),
        ],
        out_shape=[
            jax.ShapeDtypeStruct((tokens // page, 2, page, head_width), jnp.bfloat16),
            jax.ShapeDtypeStruct((heads, 2, tokens, HD), jnp.bfloat16),
        ],
        scratch_shapes=[
            pltpu.VMEM((rows, head_width), jnp.float32),
            pltpu.VMEM((rows, head_width), jnp.float32),
        ],
        compiler_params=pltpu.CompilerParams(vmem_limit_bytes=VMEM_BYTES),
        cost_estimate=pl.CostEstimate(
            flops=4 * tokens * width * head_width,
            bytes_accessed=2 * tokens * width + 4 * width * head_width,
            transcendentals=0,
        ),
        name="project",
    )(x, gain, wk, wv, cosine, sine)


ROWS = 16


def attend_kernel(
    scalars, q_ref, new_ref, kv_ref, slot_row_ref, slot_col_ref, cos_ref, sin_ref, out_ref,
    rotated, acc, done,
):
    prompt, length = scalars[1], scalars[2]
    steps, requests, width = q_ref.shape
    group = width // HD
    sources, _, span, _ = kv_ref.shape
    rows = steps * group * ROWS
    score_scale = HD ** (-0.5)

    hit_row = slot_row_ref[...] == prompt
    hit_col = slot_col_ref[...] == prompt
    square = (requests, requests)
    first = lax.broadcasted_iota(jnp.int32, square, 0)
    second = lax.broadcasted_iota(jnp.int32, square, 1)
    rank_row = jnp.sum(
        jnp.where(hit_col & (first < second), 1.0, 0.0), axis=0, keepdims=True
    ).astype(jnp.int32)
    rank_col = jnp.sum(
        jnp.where(hit_row & (second < first), 1.0, 0.0), axis=1, keepdims=True
    ).astype(jnp.int32)
    count = jnp.sum(jnp.where(hit_row, 1.0, 0.0)).astype(jnp.int32)
    done[...] = jnp.zeros_like(done)
    chunks = (length + span - 1) // span

    def tile(k, carry):
        want = k * ROWS + lax.broadcasted_iota(jnp.int32, (ROWS, requests), 0)
        pick = jnp.where((rank_row == want) & hit_row, 1.0, 0.0).astype(jnp.bfloat16)
        fresh_keys, fresh_values = [], []
        for t in range(steps):
            cosine, sine = cos_ref[t : t + 1, :], sin_ref[t : t + 1, :]
            picked = jnp.dot(pick, q_ref[t], preferred_element_type=jnp.float32)
            for g in range(group):
                head = turn(picked[:, g * HD : (g + 1) * HD], cosine, sine)
                at = (t * group + g) * ROWS
                rotated[at : at + ROWS, :] = head.astype(jnp.bfloat16)
            picked = jnp.dot(pick, new_ref[0, t], preferred_element_type=jnp.float32)
            fresh_keys.append(turn(picked, cosine, sine).astype(jnp.bfloat16))
            picked = jnp.dot(pick, new_ref[1, t], preferred_element_type=jnp.float32)
            fresh_values.append(picked.astype(jnp.bfloat16))
        fresh_keys = jnp.concatenate(fresh_keys, axis=0)
        fresh_values = jnp.concatenate(fresh_values, axis=0)
        scores = score_scale * lax.dot_general(
            rotated[...], fresh_keys, (((1,), (1,)), ((), ())), preferred_element_type=jnp.float32
        )
        row = lax.broadcasted_iota(jnp.int32, scores.shape, 0)
        column = lax.broadcasted_iota(jnp.int32, scores.shape, 1)
        allowed = (row % ROWS == column % ROWS) & (column // ROWS <= row // (group * ROWS))
        peak = jnp.max(jnp.where(allowed, scores, -1e30), axis=1, keepdims=True)
        weights = jnp.where(allowed, jnp.exp(scores - peak), 0.0)
        total = jnp.sum(weights, axis=1, keepdims=True)
        acc[...] = jnp.dot(
            weights.astype(jnp.bfloat16), fresh_values, preferred_element_type=jnp.float32
        )

        def chunk(c, state):
            peak, total = state
            scores = score_scale * lax.dot_general(
                rotated[...], kv_ref[c, 0], (((1,), (1,)), ((), ())),
                preferred_element_type=jnp.float32,
            )
            position = c * span + lax.broadcasted_iota(jnp.int32, (1, span), 1)
            scores = jnp.where(position < length, scores, -1e30)
            new_peak = jnp.maximum(peak, jnp.max(scores, axis=1, keepdims=True))
            weights = jnp.exp(scores - new_peak)
            factor = jnp.exp(peak - new_peak)
            total = total * factor + jnp.sum(weights, axis=1, keepdims=True)
            acc[...] = acc[...] * factor + jnp.dot(
                weights.astype(jnp.bfloat16), kv_ref[c, 1], preferred_element_type=jnp.float32
            )
            return new_peak, total

        peak, total = lax.fori_loop(0, chunks, chunk, (peak, total))
        result = (acc[...] / total).astype(jnp.bfloat16)
        here = pl.ds(pl.multiple_of(k * ROWS, ROWS), ROWS)
        for t in range(steps):
            for g in range(group):
                at = (t * group + g) * ROWS
                done[t, here, g * HD : (g + 1) * HD] = result[at : at + ROWS]
        return carry

    lax.fori_loop(0, (count + ROWS - 1) // ROWS, tile, 0)
    place = jnp.where((rank_col == second) & hit_col, 1.0, 0.0).astype(jnp.bfloat16)
    owned = out_ref.shape[2]
    for t in range(steps):
        spread = jnp.dot(place, done[t], preferred_element_type=jnp.float32)
        for d in range(out_ref.shape[0]):
            out_ref[d, t] = spread[d * owned : (d + 1) * owned].astype(jnp.bfloat16)


def attend(scalars, queries, new_kv, kv, slots, cosine, sine, shards, seq_count, fresh_split):
    steps, requests, query_width = queries.shape
    width = query_width // seq_count
    rows = steps * (width // HD) * ROWS
    padded = -(-requests // ROWS) * ROWS
    whole = lambda shape: pl.BlockSpec(shape, lambda i, s: (0,) * len(shape))
    fresh_index = (lambda i, s: (0, 0, 0, s[0])) if fresh_split else (lambda i, s: (0, 0, 0, 0))
    return pl.pallas_call(
        attend_kernel,
        grid_spec=pltpu.PrefetchScalarGridSpec(
            num_scalar_prefetch=1,
            grid=(1,),
            in_specs=[
                pl.BlockSpec((steps, requests, width), lambda i, s: (0, 0, s[0])),
                pl.BlockSpec((2, steps, requests, HD), fresh_index),
                whole(kv.shape),
                whole((1, requests)),
                whole((requests, 1)),
                whole(cosine.shape),
                whole(sine.shape),
            ],
            out_specs=whole((shards, steps, requests // shards, width)),
            scratch_shapes=[
                pltpu.VMEM((rows, HD), jnp.bfloat16),
                pltpu.VMEM((rows, HD), jnp.float32),
                pltpu.VMEM((steps, padded, width), jnp.bfloat16),
            ],
        ),
        out_shape=jax.ShapeDtypeStruct(
            (shards, steps, requests // shards, width), jnp.bfloat16
        ),
        compiler_params=pltpu.CompilerParams(vmem_limit_bytes=VMEM_BYTES),
        cost_estimate=pl.CostEstimate(
            flops=steps * requests * width * kv.shape[0] * kv.shape[2],
            bytes_accessed=8 * 1024 * 1024,
            transcendentals=0,
        ),
        name="attend",
    )(scalars, queries, new_kv, kv, slots[None, :], slots[:, None], cosine, sine)


def body(
    prompt_x,
    norm_gain,
    key_weight,
    value_weight,
    prompt_lengths,
    page_table,
    request_slots,
    queries,
    new_kv,
):
    seq_count = lax.axis_size("seq")
    rep_count = lax.axis_size("rep")
    tp_count = lax.axis_size("tp")
    rep_index = lax.axis_index("rep")
    seq_index = lax.axis_index("seq")
    tp_index = lax.axis_index("tp")
    shard_index = rep_index * seq_count + seq_index
    shard_count = rep_count * seq_count
    tokens = prompt_x.shape[1]
    prompts, blocks_per_prompt = page_table.shape
    pages_here = blocks_per_prompt // seq_count
    page = tokens // pages_here
    copies = max(1, tp_count // KVH)
    key_cols, value_cols = key_weight, value_weight
    if tp_count > KVH:
        other_key, other_value = swapped((key_weight, value_weight), "tp", 0)
        low_half = tp_index % 2 == 0
        key_cols = jnp.where(
            low_half,
            jnp.concatenate([key_weight, other_key], 1),
            jnp.concatenate([other_key, key_weight], 1),
        )
        value_cols = jnp.where(
            low_half,
            jnp.concatenate([value_weight, other_value], 1),
            jnp.concatenate([other_value, value_weight], 1),
        )
    head_width = key_cols.shape[1]
    heads_here = head_width // HD
    head_start = tp_index * heads_here // copies

    own_new = lax.dynamic_slice_in_dim(new_kv, head_start * HD, head_width, 3)
    all_new = lax.all_gather(own_new, ("rep", "seq"), axis=2, tiled=True)

    token_pos = (seq_index * tokens + jnp.arange(tokens, dtype=jnp.int32)).astype(jnp.float32)
    cosine, sine = rope_tables(token_pos)
    pages, heads = project(
        prompt_x[0], norm_gain[None, :], key_cols, value_cols, cosine, sine, page
    )

    by_head = heads_here == seq_count
    if by_head:
        kv = lax.all_to_all(heads, "seq", split_axis=0, concat_axis=0, tiled=True)
    else:
        kv = lax.all_gather(heads, "seq", axis=0, tiled=True)

    own_pages = lax.dynamic_slice(page_table, (rep_index, seq_index * pages_here), (1, pages_here))[0]
    hits = (
        own_pages[None, :] // pages_here == jnp.arange(shard_count, dtype=jnp.int32)[:, None]
    ).astype(jnp.int32)
    chosen = jnp.sum(hits * jnp.arange(pages_here, dtype=jnp.int32)[None, :], axis=1)
    outgoing = jnp.take(pages, chosen, axis=0, mode="clip")
    arrived = lax.all_to_all(outgoing, ("rep", "seq"), split_axis=0, concat_axis=0, tiled=True)
    page_ids = shard_index * pages_here + jnp.arange(pages_here, dtype=jnp.int32)
    flat_source = jnp.arange(prompts * blocks_per_prompt, dtype=jnp.int32) // pages_here
    matches = (page_table.reshape(-1)[None, :] == page_ids[:, None]).astype(jnp.int32)
    sources = jnp.sum(matches * flat_source[None, :], axis=1)
    paged_cache = jnp.take(arrived, sources, axis=0, mode="clip")

    own_length = lax.dynamic_index_in_dim(prompt_lengths, rep_index, 0, keepdims=False)
    steps = queries.shape[0]
    step_pos = (own_length + jnp.arange(steps, dtype=jnp.int32)).astype(jnp.float32)
    step_cos, step_sin = rope_tables(step_pos)
    scalars = jnp.stack([seq_index, rep_index, own_length]).astype(jnp.int32)
    partial = attend(
        scalars, queries, all_new, kv, request_slots, step_cos, step_sin, shard_count, seq_count,
        by_head,
    )
    owned = lax.all_to_all(partial, ("rep", "seq"), split_axis=0, concat_axis=0, tiled=True)
    attention = jnp.concatenate(
        [
            functools.reduce(
                jnp.add, [owned[r * seq_count + s] for r in range(rep_count)]
            )
            for s in range(seq_count)
        ],
        axis=-1,
    )
    return (attention, paged_cache)


def solution(mesh):
    in_specs = (
        P("rep", "seq", None),
        P(),
        P(None, "tp"),
        P(None, "tp"),
        P(),
        P(),
        P(),
        P(None, None, "tp"),
        P(None, None, ("rep", "seq"), None),
    )
    out_specs = (P(None, ("rep", "seq"), "tp"), P(("rep", "seq"), None, None, "tp"))
    return jax.shard_map(body, mesh=mesh, in_specs=in_specs, out_specs=out_specs, check_vma=False)
```
